32 devices in a mesh: blk: 16 (over z, x, core), tm: 2 (over y).
Axes of the slice: x: 2, y: 2, z: 4, core: 2. Of those that a mesh axis runs over, the one named last changes fastest.
Arguments:
- returns: bfloat16 [8192, 512], P('blk', 'tm'), may hold values from -6 to 6
- plan: int32 [2, 16], replicated, may hold values from 0 to 15, as said below
- pair_mask: int32 [16, 16], replicated, may hold values 0 or 1
Outputs:
- lead_lag: bfloat16 [8192, 2, 7680], P(('blk', 'tm'))
The draws below stay inside these ranges and needn't reach their ends.
Inputs may be any that keep to these rules, and one draw needn't show every extreme that they name: Each round r has a word m_r with plan[r, b] = b XOR m_r for every block b; m_r is never 0, and every bit of a block index is set in the word of some round.
All inputs are finite; a program needn't handle non-finite values.
Results may differ from the reference program's by a relative error of at most 0.001.
Values may be sent and summed in bfloat16 or wider, within the bound.
A program may use at most 64 MiB of HBM per device.

```python
import jax
import jax.numpy as jnp
from jax import lax

BLK = 512
LAG = 7
LAGS = 15
ROUNDS = 2
NBLOCKS = 16
NI = 8192
NT = 512


def draw_plan(key, part):
    first = jax.random.randint(key, (), 1, NBLOCKS - 1)
    rounds_idx = jnp.arange(ROUNDS)
    words = jnp.where(rounds_idx % 2 == 0, first, jnp.bitwise_xor(first, NBLOCKS - 1))
    indices = jnp.arange(NBLOCKS)
    return jnp.bitwise_xor(indices[None, :], words[:, None]).astype(jnp.int32)


def with_ends(values, rng, smallest, largest):
    shape = values.shape
    index_at = [jax.random.randint(jax.random.fold_in(rng, axis), (), 0, shape[axis]) for axis in range(len(shape))]
    values = values.at[tuple(index_at)].set(smallest)
    longest = shape.index(max(shape))
    index_at[longest] = (index_at[longest] + 1) % shape[longest]
    return values.at[tuple(index_at)].set(largest)


def steps_of(stream_key, shape, pieces, low, top_value):
    gain = 1.0
    for position, shards_of in pieces:
        steps = jax.random.uniform(jax.random.fold_in(jax.random.fold_in(stream_key, 6), position), (shards_of,), jnp.float32, low / len(pieces), top_value / len(pieces))
        gain = gain * jnp.repeat(jnp.exp(steps), shape[position] // shards_of).reshape((-1,) + (1,) * (len(shape) - 1 - position))
    return gain


def noise(rng, extent, width, reach, split=(), kind=jnp.bfloat16):
    level = steps_of(rng, extent, split, -0.22, 0.18) if split else 1.0
    entries = jax.random.normal(rng, extent, jnp.float32) * width * level
    return jnp.minimum(jnp.maximum(entries, -reach), reach).astype(kind)


def setup_inputs(seed: int = 0) -> dict:
    keys = jax.random.split(jax.random.key(seed), 4)
    return {
        "returns": noise(keys[0], (NI, NT), 1.0, 6.0, ((0, 16), (1, 2))),
        "plan": draw_plan(jax.random.fold_in(keys[3], 71), 0),
        "pair_mask": with_ends((jax.random.randint(keys[2], (NBLOCKS, NBLOCKS), 0, 4) < 3).astype(jnp.int32), jax.random.fold_in(keys[2], 1), 0, 1),
    }


def block_gram(returns, partner_of, live_of, block_idx):
    partner = partner_of[block_idx]
    own_rows = lax.dynamic_slice(returns, (block_idx * BLK, jnp.int32(0)), (BLK, NT))
    mate_rows = lax.dynamic_slice(returns, (partner * BLK, jnp.int32(0)), (BLK, NT))
    padded = jnp.pad(mate_rows, ((0, 0), (LAG, LAG)))
    stacked = jnp.concatenate([padded[:, offset:offset + NT] for offset in range(2 * LAG + 1)], axis=0)
    gram = lax.dot_general(own_rows, stacked, (((1,), (1,)), ((), ())), preferred_element_type=jnp.float32)
    weight = live_of[block_idx].astype(jnp.float32) * (float(NT) ** -0.5)
    return (gram * weight).astype(jnp.bfloat16)


def reference(returns, plan, pair_mask):
    collected = []
    indices = jnp.arange(NBLOCKS, dtype=jnp.int32)
    for round_id in range(ROUNDS):
        partner_of = plan[round_id].astype(jnp.int32)
        live_of = pair_mask[indices, partner_of]
        grams = lax.map(lambda block_idx: block_gram(returns, partner_of, live_of, block_idx), indices)
        collected.append(grams.reshape(NI, LAGS * BLK))
    return jnp.stack(collected, axis=1)
```

```python
import functools

import jax
import jax.numpy as jnp
from jax import lax
from jax.experimental import pallas as pl
from jax.experimental.pallas import tpu as pltpu
from jax.experimental.layout import Layout, with_layout_constraint
from jax.sharding import PartitionSpec as P

LAG = 7
LAGS = 2 * LAG + 1
ROUNDS = 2
LANES = 128


def swapped(block, axis, stride):
    count = lax.axis_size(axis)
    route = []
    for low in range(count):
        high = low | 1 << stride
        if high != low and high < count:
            route += [(low, high), (high, low)]
    return lax.ppermute(block, axis, route)


def gram_kernel(bi, own_ref, first_ref, second_ref, scale_ref, out_ref, mates, lhs, packed):
    slabs, rows, minutes = own_ref.shape
    width = mates.shape[1]
    total = slabs * minutes
    step = pl.program_id(0)
    groups = width // LANES
    pitch = LAGS * groups * ROUNDS

    @pl.when(step == 0)
    def _():
        for s in range(slabs):
            mates[0, :, s * minutes:(s + 1) * minutes] = first_ref[s]
            mates[1, :, s * minutes:(s + 1) * minutes] = second_ref[s]

    start = pl.multiple_of(step * bi, bi)
    own = jnp.concatenate([own_ref[s, pl.ds(start, bi), :] for s in range(slabs)], axis=1)
    own = own.astype(jnp.float32)
    lane = lax.broadcasted_iota(jnp.int32, (bi, total), 1)
    for k in range(LAGS):
        lag = k - LAG
        if lag == 0:
            moved = own
        else:
            moved = pltpu.roll(own, lag % total, 1)
            keep = lane >= lag if lag > 0 else lane < total + lag
            moved = jnp.where(keep, moved, 0.0)
        lhs[k * bi:(k + 1) * bi, :] = moved.astype(lhs.dtype)
    for r in range(ROUNDS):
        gram = lax.dot_general(
            lhs[...], mates[r], (((1,), (1,)), ((), ())), preferred_element_type=jnp.float32
        ) * scale_ref[r]
        for k in range(LAGS):
            for c in range(groups):
                packed[pl.ds((k * groups + c) * ROUNDS + r, bi, stride=pitch), :] = gram[
                    k * bi:(k + 1) * bi, c * LANES:(c + 1) * LANES
                ]
    out_ref[...] = packed[...].astype(out_ref.dtype)


def gram_call(own, first, second, scale):
    slabs, rows, minutes = own.shape
    width = first.shape[1]
    total = slabs * minutes
    bi = min(32, rows)
    pitch = LAGS * (width // LANES) * ROUNDS
    whole = lambda a: pl.BlockSpec(a.shape, lambda i: (0, 0, 0))
    flat = pl.pallas_call(
        functools.partial(gram_kernel, bi),
        grid=(rows // bi,),
        in_specs=[
            whole(own), whole(first), whole(second),
            pl.BlockSpec(memory_space=pltpu.SMEM),
        ],
        out_specs=pl.BlockSpec((bi * pitch, LANES), lambda i: (i, 0)),
        out_shape=jax.ShapeDtypeStruct((rows * pitch, LANES), jnp.bfloat16),
        scratch_shapes=[
            pltpu.VMEM((ROUNDS, width, total), jnp.bfloat16),
            pltpu.VMEM((LAGS * bi, total), jnp.bfloat16),
            pltpu.VMEM((bi * pitch, LANES), jnp.float32),
        ],
        compiler_params=pltpu.CompilerParams(vmem_limit_bytes=48 * 2**20),
    )(own, first, second, scale)
    tiles = flat.reshape(rows, pitch // ROUNDS, ROUNDS, LANES)
    tiles = with_layout_constraint(tiles, Layout(major_to_minor=(0, 1, 2, 3)))
    return tiles.transpose(0, 2, 1, 3).reshape(rows, ROUNDS, LAGS * width)


def on_device(returns, plan, pair_mask):
    own_block = lax.axis_index("blk")
    bit_count = lax.axis_size("blk").bit_length() - 1
    slab_count = lax.axis_size("tm")
    width, minutes = returns.shape
    factor = float(minutes * slab_count) ** (-0.5)
    own = lax.all_to_all(
        returns.reshape(slab_count, width // slab_count, minutes), "tm", split_axis=0, concat_axis=0
    )
    mates, scales = [], []
    for round_id in range(ROUNDS):
        mask_word = plan[round_id, 0]
        partner = jnp.bitwise_xor(own_block, mask_word)
        scales.append(factor * pair_mask[own_block, partner].astype(jnp.float32))
        current = returns
        for bit in range(bit_count):
            flag = jnp.bitwise_and(jnp.right_shift(mask_word, bit), 1)
            arrived = swapped(current, "blk", bit)
            current = jnp.where(flag == 1, arrived, current)
        mates.append(lax.all_gather(current, "tm", axis=0))
    return gram_call(own, mates[0], mates[1], jnp.stack(scales))


def solution(mesh):
    in_specs = (P("blk", "tm"), P(), P())
    out_specs = P(("blk", "tm"), None, None)
    return jax.shard_map(
        on_device, mesh=mesh, in_specs=in_specs, out_specs=out_specs, check_vma=False
    )
```

```python
import functools

import jax
import jax.numpy as jnp
import numpy as np
from jax import lax
from jax.experimental import pallas as pl
from jax.experimental.pallas import tpu as pltpu
from jax.experimental.layout import Layout, with_layout_constraint
from jax.sharding import PartitionSpec as P

LAG = 7
LAGS = 2 * LAG + 1
ROUNDS = 2
LANES = 128


CHUNKS = 4


def word_pairs(count):
    return [
        (low, high)
        for low in range(1, count)
        for high in range(low, count)
        if low | high == count - 1
    ]


def flipped(block, word):
    bit, partner = 1, block
    while bit <= word:
        if word & bit:
            partner = partner + bit - 2 * bit * ((block // bit) % 2)
        bit *= 2
    return partner


def exchange_kernel(
    words, slabs, top, source, own, mates,
    local_sem, own_send, own_recv, far_send, far_recv, near_send, near_recv,
):
    block, slab = lax.axis_index("blk"), lax.axis_index("tm")
    width = source.shape[0]
    rows = width // slabs
    depth = width // CHUNKS

    def sibling(offset):
        return (slab + offset) % slabs

    def own_copy(offset, writer):
        reader = sibling(offset)
        return pltpu.make_async_remote_copy(
            src_ref=source.at[pl.ds(pl.multiple_of(reader * rows, rows), rows)],
            dst_ref=own.at[writer],
            send_sem=own_send.at[offset - 1],
            recv_sem=own_recv.at[offset - 1],
            device_id=(block, reader),
            device_id_type=pl.DeviceIdType.MESH,
        )

    def far_copy(r, c):
        return pltpu.make_async_remote_copy(
            src_ref=source.at[pl.ds(c * depth, depth)],
            dst_ref=mates.at[r, slab, pl.ds(c * depth, depth)],
            send_sem=far_send.at[r, c],
            recv_sem=far_recv.at[r, c],
            device_id=(flipped(block, words[r]), slab),
            device_id_type=pl.DeviceIdType.MESH,
        )

    def near_copy(r, c, offset, writer):
        part = pl.ds(c * depth, depth)
        return pltpu.make_async_remote_copy(
            src_ref=mates.at[r, slab, part],
            dst_ref=mates.at[r, writer, part],
            send_sem=near_send.at[r, c, offset - 1],
            recv_sem=near_recv.at[r, c, offset - 1],
            device_id=(block, sibling(offset)),
            device_id_type=pl.DeviceIdType.MESH,
        )

    pieces = [
        (1 + c if word < top else 2 * (1 + c), r, c)
        for r, word in enumerate(words)
        for c in range(CHUNKS)
    ]
    pieces.sort()
    offsets = range(1, slabs)
    for _, r, c in pieces:
        far_copy(r, c).start()
    for offset in offsets:
        own_copy(offset, slab).start()
    local = pltpu.make_async_copy(
        source.at[pl.ds(pl.multiple_of(slab * rows, rows), rows)], own.at[slab], local_sem
    )
    local.start()
    for _, r, c in pieces:
        far_copy(r, c).wait_recv()
        for offset in offsets:
            near_copy(r, c, offset, slab).start()
    local.wait()
    for offset in offsets:
        own_copy(offset, slab).wait_send()
        own_copy(offset, sibling(slabs - offset)).wait_recv()
    for _, r, c in pieces:
        far_copy(r, c).wait_send()
        for offset in offsets:
            near_copy(r, c, offset, slab).wait_send()
            near_copy(r, c, offset, sibling(slabs - offset)).wait_recv()


def exchange_call(words, slabs, top, returns):
    width, minutes = returns.shape
    vmem = pl.BlockSpec(memory_space=pltpu.VMEM)
    dma = pltpu.SemaphoreType.DMA
    return pl.pallas_call(
        functools.partial(exchange_kernel, words, slabs, top),
        in_specs=[vmem],
        out_specs=[vmem, vmem],
        out_shape=[
            jax.ShapeDtypeStruct((slabs, width // slabs, minutes), returns.dtype),
            jax.ShapeDtypeStruct((ROUNDS, slabs, width, minutes), returns.dtype),
        ],
        scratch_shapes=[
            dma(()), dma((slabs - 1,)), dma((slabs - 1,)),
            dma((ROUNDS, CHUNKS)), dma((ROUNDS, CHUNKS)),
            dma((ROUNDS, CHUNKS, slabs - 1)), dma((ROUNDS, CHUNKS, slabs - 1)),
        ],
        compiler_params=pltpu.CompilerParams(has_side_effects=True),
    )(returns)


def gram_kernel(bi, own_ref, mates_ref, swap_ref, scale_ref, out_ref, mates, lhs, packed):
    slabs, rows, minutes = own_ref.shape
    width = mates.shape[1]
    total = slabs * minutes
    step = pl.program_id(0)
    groups = width // LANES
    pitch = LAGS * groups * ROUNDS

    @pl.when(step == 0)
    def _():
        for s in range(slabs):
            for r in range(ROUNDS):
                mates[r, :, s * minutes:(s + 1) * minutes] = mates_ref[r, s]

    start = pl.multiple_of(step * bi, bi)
    own = jnp.concatenate([own_ref[s, pl.ds(start, bi), :] for s in range(slabs)], axis=1)
    own = own.astype(jnp.float32)
    lane = lax.broadcasted_iota(jnp.int32, (bi, total), 1)
    for k in range(LAGS):
        lag = k - LAG
        if lag == 0:
            moved = own
        else:
            moved = pltpu.roll(own, lag % total, 1)
            keep = lane >= lag if lag > 0 else lane < total + lag
            moved = jnp.where(keep, moved, 0.0)
        lhs[k * bi:(k + 1) * bi, :] = moved.astype(lhs.dtype)
    for r in range(ROUNDS):
        gram = lax.dot_general(
            lhs[...], mates[jnp.bitwise_xor(swap_ref[0], r)], (((1,), (1,)), ((), ())), preferred_element_type=jnp.float32
        ) * scale_ref[r]
        for k in range(LAGS):
            for c in range(groups):
                packed[pl.ds((k * groups + c) * ROUNDS + r, bi, stride=pitch), :] = gram[
                    k * bi:(k + 1) * bi, c * LANES:(c + 1) * LANES
                ]
    out_ref[...] = packed[...].astype(out_ref.dtype)


def gram_call(own, found, swap, scale):
    slabs, rows, minutes = own.shape
    width = found.shape[2]
    total = slabs * minutes
    bi = min(32, rows)
    pitch = LAGS * (width // LANES) * ROUNDS
    whole = lambda a: pl.BlockSpec(a.shape, lambda i: (0,) * a.ndim)
    flat = pl.pallas_call(
        functools.partial(gram_kernel, bi),
        grid=(rows // bi,),
        in_specs=[
            whole(own), whole(found),
            pl.BlockSpec(memory_space=pltpu.SMEM),
            pl.BlockSpec(memory_space=pltpu.SMEM),
        ],
        out_specs=pl.BlockSpec((bi * pitch, LANES), lambda i: (i, 0)),
        out_shape=jax.ShapeDtypeStruct((rows * pitch, LANES), jnp.bfloat16),
        scratch_shapes=[
            pltpu.VMEM((ROUNDS, width, total), jnp.bfloat16),
            pltpu.VMEM((LAGS * bi, total), jnp.bfloat16),
            pltpu.VMEM((bi * pitch, LANES), jnp.float32),
        ],
        compiler_params=pltpu.CompilerParams(vmem_limit_bytes=48 * 2**20),
    )(own, found, swap, scale)
    tiles = flat.reshape(rows, pitch // ROUNDS, ROUNDS, LANES)
    tiles = with_layout_constraint(tiles, Layout(major_to_minor=(0, 1, 2, 3)))
    return tiles.transpose(0, 2, 1, 3).reshape(rows, ROUNDS, LAGS * width)


def on_device(returns, plan, pair_mask):
    own_block = lax.axis_index("blk")
    block_count = lax.axis_size("blk")
    slab_count = lax.axis_size("tm")
    minutes = returns.shape[1]
    factor = float(minutes * slab_count) ** (-0.5)
    first, second = plan[0, 0], plan[1, 0]
    low, high = jnp.minimum(first, second), jnp.maximum(first, second)
    pairs = word_pairs(block_count)
    table = np.zeros((block_count, block_count), np.int32)
    for index, pair in enumerate(pairs):
        table[pair] = index
    choice = jnp.asarray(table)[low, high]
    own, found = lax.switch(
        choice,
        [
            functools.partial(exchange_call, pair, slab_count, block_count // 2)
            for pair in pairs
        ],
        returns,
    )
    swap = (first > second).astype(jnp.int32)[None]
    partners = jnp.bitwise_xor(own_block, jnp.stack([first, second]))
    scale = factor * pair_mask[own_block][partners].astype(jnp.float32)
    return gram_call(own, found, swap, scale)


def solution(mesh):
    in_specs = (P("blk", "tm"), P(), P())
    out_specs = P(("blk", "tm"), None, None)
    return jax.shard_map(
        on_device, mesh=mesh, in_specs=in_specs, out_specs=out_specs, check_vma=False
    )
```

```python
import functools

import jax
import jax.numpy as jnp
from jax import lax
from jax.experimental import pallas as pl
from jax.experimental.pallas import tpu as pltpu
from jax.experimental.layout import Layout, with_layout_constraint
from jax.sharding import PartitionSpec as P

LAG = 7
LAGS = 2 * LAG + 1
ROUNDS = 2
LANES = 128


CHUNKS = 4


def word_pairs(count):
    return [
        (low, high)
        for low in range(1, count)
        for high in range(low, count)
        if low | high == count - 1
    ]


def flipped(block, word):
    bit, partner = 1, block
    while bit <= word:
        if word & bit:
            partner = partner + bit - 2 * bit * ((block // bit) % 2)
        bit *= 2
    return partner


def exchange_kernel(
    words, slabs, top, source, own, mates,
    local_sem, own_send, own_recv, far_send, far_recv, near_send, near_recv,
):
    block, slab = lax.axis_index("blk"), lax.axis_index("tm")
    width = source.shape[0]
    rows = width // slabs
    depth = width // CHUNKS

    def sibling(offset):
        return (slab + offset) % slabs

    def own_copy(offset, writer):
        reader = sibling(offset)
        return pltpu.make_async_remote_copy(
            src_ref=source.at[pl.ds(pl.multiple_of(reader * rows, rows), rows)],
            dst_ref=own.at[writer],
            send_sem=own_send.at[offset - 1],
            recv_sem=own_recv.at[offset - 1],
            device_id=(block, reader),
            device_id_type=pl.DeviceIdType.MESH,
        )

    def far_copy(r, c):
        return pltpu.make_async_remote_copy(
            src_ref=source.at[pl.ds(c * depth, depth)],
            dst_ref=mates.at[r, slab, pl.ds(c * depth, depth)],
            send_sem=far_send.at[r, c],
            recv_sem=far_recv.at[r, c],
            device_id=(flipped(block, words[r]), slab),
            device_id_type=pl.DeviceIdType.MESH,
        )

    def near_copy(r, c, offset, writer):
        part = pl.ds(c * depth, depth)
        return pltpu.make_async_remote_copy(
            src_ref=mates.at[r, slab, part],
            dst_ref=mates.at[r, writer, part],
            send_sem=near_send.at[r, c, offset - 1],
            recv_sem=near_recv.at[r, c, offset - 1],
            device_id=(block, sibling(offset)),
            device_id_type=pl.DeviceIdType.MESH,
        )

    pieces = [
        (1 + c if word < top else 2 * (1 + c), r, c)
        for r, word in enumerate(words)
        for c in range(CHUNKS)
    ]
    pieces.sort()
    offsets = range(1, slabs)
    for _, r, c in pieces:
        far_copy(r, c).start()
    for offset in offsets:
        own_copy(offset, slab).start()
    local = pltpu.make_async_copy(
        source.at[pl.ds(pl.multiple_of(slab * rows, rows), rows)], own.at[slab], local_sem
    )
    local.start()
    for _, r, c in pieces:
        far_copy(r, c).wait_recv()
        for offset in offsets:
            near_copy(r, c, offset, slab).start()
    local.wait()
    for offset in offsets:
        own_copy(offset, slab).wait_send()
        own_copy(offset, sibling(slabs - offset)).wait_recv()
    for _, r, c in pieces:
        far_copy(r, c).wait_send()
        for offset in offsets:
            near_copy(r, c, offset, slab).wait_send()
            near_copy(r, c, offset, sibling(slabs - offset)).wait_recv()


def exchange_call(words, slabs, top, returns):
    width, minutes = returns.shape
    vmem = pl.BlockSpec(memory_space=pltpu.VMEM)
    dma = pltpu.SemaphoreType.DMA
    return pl.pallas_call(
        functools.partial(exchange_kernel, words, slabs, top),
        in_specs=[vmem],
        out_specs=[vmem, vmem],
        out_shape=[
            jax.ShapeDtypeStruct((slabs, width // slabs, minutes), returns.dtype),
            jax.ShapeDtypeStruct((ROUNDS, slabs, width, minutes), returns.dtype),
        ],
        scratch_shapes=[
            dma(()), dma((slabs - 1,)), dma((slabs - 1,)),
            dma((ROUNDS, CHUNKS)), dma((ROUNDS, CHUNKS)),
            dma((ROUNDS, CHUNKS, slabs - 1)), dma((ROUNDS, CHUNKS, slabs - 1)),
        ],
        compiler_params=pltpu.CompilerParams(has_side_effects=True),
    )(returns)


def gram_kernel(bi, own_ref, mates_ref, plan_ref, mask_ref, out_ref, mates, lhs, packed):
    slabs, rows, minutes = own_ref.shape
    width = mates.shape[1]
    total = slabs * minutes
    step = pl.program_id(0)
    block = lax.axis_index("blk")
    factor = float(total) ** (-0.5)
    swap = (plan_ref[0, 0] > plan_ref[1, 0]).astype(jnp.int32)
    groups = width // LANES
    pitch = LAGS * groups * ROUNDS

    @pl.when(step == 0)
    def _():
        for s in range(slabs):
            for r in range(ROUNDS):
                mates[r, :, s * minutes:(s + 1) * minutes] = mates_ref[r, s]

    start = pl.multiple_of(step * bi, bi)
    own = jnp.concatenate([own_ref[s, pl.ds(start, bi), :] for s in range(slabs)], axis=1)
    own = own.astype(jnp.float32)
    lane = lax.broadcasted_iota(jnp.int32, (bi, total), 1)
    for k in range(LAGS):
        lag = k - LAG
        if lag == 0:
            moved = own
        else:
            moved = pltpu.roll(own, lag % total, 1)
            keep = lane >= lag if lag > 0 else lane < total + lag
            moved = jnp.where(keep, moved, 0.0)
        lhs[k * bi:(k + 1) * bi, :] = moved.astype(lhs.dtype)
    for r in range(ROUNDS):
        partner = jnp.bitwise_xor(block, plan_ref[r, 0])
        scale = mask_ref[block, partner].astype(jnp.float32) * factor
        gram = lax.dot_general(
            lhs[...], mates[jnp.bitwise_xor(swap, r)], (((1,), (1,)), ((), ())), preferred_element_type=jnp.float32
        ) * scale
        for k in range(LAGS):
            for c in range(groups):
                packed[pl.ds((k * groups + c) * ROUNDS + r, bi, stride=pitch), :] = gram[
                    k * bi:(k + 1) * bi, c * LANES:(c + 1) * LANES
                ]
    out_ref[...] = packed[...].astype(out_ref.dtype)


def gram_call(own, found, plan, pair_mask):
    slabs, rows, minutes = own.shape
    width = found.shape[2]
    total = slabs * minutes
    bi = min(32, rows)
    pitch = LAGS * (width // LANES) * ROUNDS
    whole = lambda a: pl.BlockSpec(a.shape, lambda i: (0,) * a.ndim)
    flat = pl.pallas_call(
        functools.partial(gram_kernel, bi),
        grid=(rows // bi,),
        in_specs=[
            whole(own), whole(found),
            pl.BlockSpec(memory_space=pltpu.SMEM),
            pl.BlockSpec(memory_space=pltpu.SMEM),
        ],
        out_specs=pl.BlockSpec((bi * pitch, LANES), lambda i: (i, 0)),
        out_shape=jax.ShapeDtypeStruct((rows * pitch, LANES), jnp.bfloat16),
        scratch_shapes=[
            pltpu.VMEM((ROUNDS, width, total), jnp.bfloat16),
            pltpu.VMEM((LAGS * bi, total), jnp.bfloat16),
            pltpu.VMEM((bi * pitch, LANES), jnp.float32),
        ],
        compiler_params=pltpu.CompilerParams(vmem_limit_bytes=48 * 2**20),
    )(own, found, plan, pair_mask)
    tiles = flat.reshape(rows, pitch // ROUNDS, ROUNDS, LANES)
    tiles = with_layout_constraint(tiles, Layout(major_to_minor=(0, 1, 2, 3)))
    return tiles.transpose(0, 2, 1, 3).reshape(rows, ROUNDS, LAGS * width)


def choice_kernel(pairs, plan_ref, choice_ref):
    first, second = plan_ref[0, 0], plan_ref[1, 0]
    low, high = jnp.minimum(first, second), jnp.maximum(first, second)
    choice = jnp.int32(0)
    for index, (a, b) in enumerate(pairs):
        choice = jnp.where((low == a) & (high == b), jnp.int32(index), choice)
    choice_ref[0] = choice


def on_device(returns, plan, pair_mask):
    block_count = lax.axis_size("blk")
    slab_count = lax.axis_size("tm")
    pairs = word_pairs(block_count)
    smem = pl.BlockSpec(memory_space=pltpu.SMEM)
    choice = pl.pallas_call(
        functools.partial(choice_kernel, pairs),
        in_specs=[smem],
        out_specs=smem,
        out_shape=jax.ShapeDtypeStruct((1,), jnp.int32),
    )(plan)
    own, found = lax.switch(
        choice[0],
        [
            functools.partial(exchange_call, pair, slab_count, block_count // 2)
            for pair in pairs
        ],
        returns,
    )
    return gram_call(own, found, plan, pair_mask)


def solution(mesh):
    in_specs = (P("blk", "tm"), P(), P())
    out_specs = P(("blk", "tm"), None, None)
    return jax.shard_map(
        on_device, mesh=mesh, in_specs=in_specs, out_specs=out_specs, check_vma=False
    )
```

```python
import functools

import jax
import jax.numpy as jnp
from jax import lax
from jax.experimental import pallas as pl
from jax.experimental.pallas import tpu as pltpu
from jax.experimental.layout import Layout, with_layout_constraint
from jax.sharding import PartitionSpec as P

LAG = 7
LAGS = 2 * LAG + 1
ROUNDS = 2
LANES = 128


def chunk_count(slabs):
    return max(1, 16 // slabs)


def word_pairs(count):
    return [
        (low, high)
        for low in range(1, count)
        for high in range(low, count)
        if low | high == count - 1
    ]


def flipped(block, word):
    bit, partner = 1, block
    while bit <= word:
        if word & bit:
            partner = partner + bit - 2 * bit * ((block // bit) % 2)
        bit *= 2
    return partner


def exchange_kernel(
    words, slabs, top, source, own, mates,
    other, cross_send, cross_recv, local_sem, own_send, own_recv, far_send, far_recv, near_send, near_recv,
):
    block, slab = lax.axis_index("blk"), lax.axis_index("tm")
    width = source.shape[0]
    rows = width // slabs
    count = chunk_count(slabs)
    depth = width // count

    def sibling(offset):
        return (slab + offset) % slabs

    def own_copy(offset, writer):
        reader = sibling(offset)
        return pltpu.make_async_remote_copy(
            src_ref=source.at[pl.ds(pl.multiple_of(reader * rows, rows), rows)],
            dst_ref=own.at[writer],
            send_sem=own_send.at[offset - 1],
            recv_sem=own_recv.at[offset - 1],
            device_id=(block, reader),
            device_id_type=pl.DeviceIdType.MESH,
        )

    def far_copy(r, c):
        return pltpu.make_async_remote_copy(
            src_ref=source.at[pl.ds(c * depth, depth)],
            dst_ref=mates.at[r, slab, pl.ds(c * depth, depth)],
            send_sem=far_send.at[r, c],
            recv_sem=far_recv.at[r, c],
            device_id=(flipped(block, words[r]), slab),
            device_id_type=pl.DeviceIdType.MESH,
        )

    def near_copy(r, c, offset, writer):
        part = pl.ds(c * depth, depth)
        return pltpu.make_async_remote_copy(
            src_ref=mates.at[r, slab, part],
            dst_ref=mates.at[r, writer, part],
            send_sem=near_send.at[r, c, offset - 1],
            recv_sem=near_recv.at[r, c, offset - 1],
            device_id=(block, sibling(offset)),
            device_id_type=pl.DeviceIdType.MESH,
        )

    local = pltpu.make_async_copy(
        source.at[pl.ds(pl.multiple_of(slab * rows, rows), rows)], own.at[slab], local_sem
    )
    offsets = range(1, slabs)
    chunks = range(count)
    if slabs == 2 and words[0] < top // 2:
        reader = sibling(1)

        def cross_copy(c):
            part = pl.ds(c * depth, depth)
            return pltpu.make_async_remote_copy(
                src_ref=source.at[part],
                dst_ref=other.at[part],
                send_sem=cross_send.at[c],
                recv_sem=cross_recv.at[c],
                device_id=(block, reader),
                device_id_type=pl.DeviceIdType.MESH,
            )

        def relay_copy(c):
            part = pl.ds(c * depth, depth)
            return pltpu.make_async_remote_copy(
                src_ref=other.at[part],
                dst_ref=mates.at[0, reader, part],
                send_sem=near_send.at[0, c, 0],
                recv_sem=near_recv.at[0, c, 0],
                device_id=(flipped(block, words[0]), slab),
                device_id_type=pl.DeviceIdType.MESH,
            )

        for c in chunks:
            cross_copy(c).start()
            far_copy(1, c).start()
            far_copy(0, c).start()
        local.start()
        events = [(1 + c, 0, c) for c in chunks] + [(2 * (1 + c), 1, c) for c in chunks]
        for _, r, c in sorted(events):
            if r == 0:
                cross_copy(c).wait_recv()
                relay_copy(c).start()
            else:
                far_copy(1, c).wait_recv()
                near_copy(1, c, 1, slab).start()
        local.wait()
        local_other = pltpu.make_async_copy(
            other.at[pl.ds(pl.multiple_of(slab * rows, rows), rows)], own.at[reader], local_sem
        )
        local_other.start()
        local_other.wait()
        for c in chunks:
            cross_copy(c).wait_send()
            far_copy(0, c).wait()
            far_copy(1, c).wait_send()
            relay_copy(c).wait()
            near_copy(1, c, 1, slab).wait_send()
            near_copy(1, c, 1, reader).wait_recv()
        return

    pieces = [
        (1 + c if word < top else 2 * (1 + c), r, c)
        for r, word in enumerate(words)
        for c in chunks
    ]
    pieces.sort()
    for _, r, c in pieces:
        far_copy(r, c).start()
    for offset in offsets:
        own_copy(offset, slab).start()
    local.start()
    for _, r, c in pieces:
        far_copy(r, c).wait_recv()
        for offset in offsets:
            near_copy(r, c, offset, slab).start()
    local.wait()
    for offset in offsets:
        own_copy(offset, slab).wait_send()
        own_copy(offset, sibling(slabs - offset)).wait_recv()
    for _, r, c in pieces:
        far_copy(r, c).wait_send()
        for offset in offsets:
            near_copy(r, c, offset, slab).wait_send()
            near_copy(r, c, offset, sibling(slabs - offset)).wait_recv()


def exchange_call(words, slabs, top, returns):
    width, minutes = returns.shape
    count = chunk_count(slabs)
    vmem = pl.BlockSpec(memory_space=pltpu.VMEM)
    dma = pltpu.SemaphoreType.DMA
    return pl.pallas_call(
        functools.partial(exchange_kernel, words, slabs, top),
        in_specs=[vmem],
        out_specs=[vmem, vmem],
        out_shape=[
            jax.ShapeDtypeStruct((slabs, width // slabs, minutes), returns.dtype),
            jax.ShapeDtypeStruct((ROUNDS, slabs, width, minutes), returns.dtype),
        ],
        scratch_shapes=[
            pltpu.VMEM((width, minutes), returns.dtype), dma((count,)), dma((count,)),
            dma(()), dma((slabs - 1,)), dma((slabs - 1,)),
            dma((ROUNDS, count)), dma((ROUNDS, count)),
            dma((ROUNDS, count, slabs - 1)), dma((ROUNDS, count, slabs - 1)),
        ],
        compiler_params=pltpu.CompilerParams(has_side_effects=True),
    )(returns)


def gram_kernel(bi, own_ref, mates_ref, plan_ref, mask_ref, out_ref, mates, lhs, packed):
    slabs, rows, minutes = own_ref.shape
    width = mates.shape[1]
    total = slabs * minutes
    step = pl.program_id(0)
    block = lax.axis_index("blk")
    factor = float(total) ** (-0.5)
    swap = (plan_ref[0, 0] > plan_ref[1, 0]).astype(jnp.int32)
    groups = width // LANES
    pitch = LAGS * groups * ROUNDS

    @pl.when(step == 0)
    def _():
        for s in range(slabs):
            for r in range(ROUNDS):
                mates[r, :, s * minutes:(s + 1) * minutes] = mates_ref[r, s]

    start = pl.multiple_of(step * bi, bi)
    own = jnp.concatenate([own_ref[s, pl.ds(start, bi), :] for s in range(slabs)], axis=1)
    own = own.astype(jnp.float32)
    lane = lax.broadcasted_iota(jnp.int32, (bi, total), 1)
    for k in range(LAGS):
        lag = k - LAG
        if lag == 0:
            moved = own
        else:
            moved = pltpu.roll(own, lag % total, 1)
            keep = lane >= lag if lag > 0 else lane < total + lag
            moved = jnp.where(keep, moved, 0.0)
        lhs[k * bi:(k + 1) * bi, :] = moved.astype(lhs.dtype)
    for r in range(ROUNDS):
        partner = jnp.bitwise_xor(block, plan_ref[r, 0])
        scale = mask_ref[block, partner].astype(jnp.float32) * factor
        gram = lax.dot_general(
            lhs[...], mates[jnp.bitwise_xor(swap, r)], (((1,), (1,)), ((), ())), preferred_element_type=jnp.float32
        ) * scale
        for k in range(LAGS):
            for c in range(groups):
                packed[pl.ds((k * groups + c) * ROUNDS + r, bi, stride=pitch), :] = gram[
                    k * bi:(k + 1) * bi, c * LANES:(c + 1) * LANES
                ]
    out_ref[...] = packed[...].astype(out_ref.dtype)


def gram_call(own, found, plan, pair_mask):
    slabs, rows, minutes = own.shape
    width = found.shape[2]
    total = slabs * minutes
    bi = min(32, rows)
    pitch = LAGS * (width // LANES) * ROUNDS
    whole = lambda a: pl.BlockSpec(a.shape, lambda i: (0,) * a.ndim)
    flat = pl.pallas_call(
        functools.partial(gram_kernel, bi),
        grid=(rows // bi,),
        in_specs=[
            whole(own), whole(found),
            pl.BlockSpec(memory_space=pltpu.SMEM),
            pl.BlockSpec(memory_space=pltpu.SMEM),
        ],
        out_specs=pl.BlockSpec((bi * pitch, LANES), lambda i: (i, 0)),
        out_shape=jax.ShapeDtypeStruct((rows * pitch, LANES), jnp.bfloat16),
        scratch_shapes=[
            pltpu.VMEM((ROUNDS, width, total), jnp.bfloat16),
            pltpu.VMEM((LAGS * bi, total), jnp.bfloat16),
            pltpu.VMEM((bi * pitch, LANES), jnp.float32),
        ],
        compiler_params=pltpu.CompilerParams(vmem_limit_bytes=48 * 2**20),
    )(own, found, plan, pair_mask)
    tiles = flat.reshape(rows, pitch // ROUNDS, ROUNDS, LANES)
    tiles = with_layout_constraint(tiles, Layout(major_to_minor=(0, 1, 2, 3)))
    return tiles.transpose(0, 2, 1, 3).reshape(rows, ROUNDS, LAGS * width)


def choice_kernel(pairs, plan_ref, choice_ref):
    first, second = plan_ref[0, 0], plan_ref[1, 0]
    low, high = jnp.minimum(first, second), jnp.maximum(first, second)
    choice = jnp.int32(0)
    for index, (a, b) in enumerate(pairs):
        choice = jnp.where((low == a) & (high == b), jnp.int32(index), choice)
    choice_ref[0] = choice


def on_device(returns, plan, pair_mask):
    block_count = lax.axis_size("blk")
    slab_count = lax.axis_size("tm")
    pairs = word_pairs(block_count)
    smem = pl.BlockSpec(memory_space=pltpu.SMEM)
    choice = pl.pallas_call(
        functools.partial(choice_kernel, pairs),
        in_specs=[smem],
        out_specs=smem,
        out_shape=jax.ShapeDtypeStruct((1,), jnp.int32),
    )(plan)
    own, found = lax.switch(
        choice[0],
        [
            functools.partial(exchange_call, pair, slab_count, block_count // 2)
            for pair in pairs
        ],
        returns,
    )
    return gram_call(own, found, plan, pair_mask)


def solution(mesh):
    in_specs = (P("blk", "tm"), P(), P())
    out_specs = P(("blk", "tm"), None, None)
    return jax.shard_map(
        on_device, mesh=mesh, in_specs=in_specs, out_specs=out_specs, check_vma=False
    )
```

```python
import functools

import jax
import jax.numpy as jnp
from jax import lax
from jax.experimental import pallas as pl
from jax.experimental.pallas import tpu as pltpu
from jax.experimental.layout import Layout, with_layout_constraint
from jax.sharding import PartitionSpec as P

LAG = 7
LAGS = 2 * LAG + 1
ROUNDS = 2
LANES = 128


def chunk_count(slabs):
    return max(1, 16 // slabs)


def word_pairs(count):
    return [
        (low, high)
        for low in range(1, count)
        for high in range(low, count)
        if low | high == count - 1
    ]


def flipped(block, word):
    bit, partner = 1, block
    while bit <= word:
        if word & bit:
            partner = partner + bit - 2 * bit * ((block // bit) % 2)
        bit *= 2
    return partner


def exchange_kernel(
    words, slabs, top, source, own, mates,
    other, cross_send, cross_recv, local_sem, own_send, own_recv, far_send, far_recv, near_send, near_recv,
):
    block, slab = lax.axis_index("blk"), lax.axis_index("tm")
    width = source.shape[0]
    rows = width // slabs
    count = chunk_count(slabs)
    depth = width // count

    def sibling(offset):
        return (slab + offset) % slabs

    def own_copy(offset, writer):
        reader = sibling(offset)
        return pltpu.make_async_remote_copy(
            src_ref=source.at[pl.ds(pl.multiple_of(reader * rows, rows), rows)],
            dst_ref=own.at[writer],
            send_sem=own_send.at[offset - 1],
            recv_sem=own_recv.at[offset - 1],
            device_id=(block, reader),
            device_id_type=pl.DeviceIdType.MESH,
        )

    def far_copy(r, c):
        return pltpu.make_async_remote_copy(
            src_ref=source.at[pl.ds(c * depth, depth)],
            dst_ref=mates.at[r, slab, pl.ds(c * depth, depth)],
            send_sem=far_send.at[r, c],
            recv_sem=far_recv.at[r, c],
            device_id=(flipped(block, words[r]), slab),
            device_id_type=pl.DeviceIdType.MESH,
        )

    def near_copy(r, c, offset, writer):
        part = pl.ds(c * depth, depth)
        return pltpu.make_async_remote_copy(
            src_ref=mates.at[r, slab, part],
            dst_ref=mates.at[r, writer, part],
            send_sem=near_send.at[r, c, offset - 1],
            recv_sem=near_recv.at[r, c, offset - 1],
            device_id=(block, sibling(offset)),
            device_id_type=pl.DeviceIdType.MESH,
        )

    local = pltpu.make_async_copy(
        source.at[pl.ds(pl.multiple_of(slab * rows, rows), rows)], own.at[slab], local_sem
    )
    offsets = range(1, slabs)
    chunks = range(count)
    if slabs == 2 and words[0] < top // 2:
        reader = sibling(1)

        def cross_copy(c):
            part = pl.ds(c * depth, depth)
            return pltpu.make_async_remote_copy(
                src_ref=source.at[part],
                dst_ref=other.at[part],
                send_sem=cross_send.at[c],
                recv_sem=cross_recv.at[c],
                device_id=(block, reader),
                device_id_type=pl.DeviceIdType.MESH,
            )

        def relay_copy(c):
            part = pl.ds(c * depth, depth)
            return pltpu.make_async_remote_copy(
                src_ref=other.at[part],
                dst_ref=mates.at[0, reader, part],
                send_sem=near_send.at[0, c, 0],
                recv_sem=near_recv.at[0, c, 0],
                device_id=(flipped(block, words[0]), slab),
                device_id_type=pl.DeviceIdType.MESH,
            )

        for c in chunks:
            cross_copy(c).start()
            far_copy(1, c).start()
            far_copy(0, c).start()
        local.start()
        events = [(1 + c, 0, c) for c in chunks] + [(2 * (1 + c), 1, c) for c in chunks]
        for _, r, c in sorted(events):
            if r == 0:
                cross_copy(c).wait_recv()
                relay_copy(c).start()
            else:
                far_copy(1, c).wait_recv()
                near_copy(1, c, 1, slab).start()
        local.wait()
        local_other = pltpu.make_async_copy(
            other.at[pl.ds(pl.multiple_of(slab * rows, rows), rows)], own.at[reader], local_sem
        )
        local_other.start()
        local_other.wait()
        for c in chunks:
            cross_copy(c).wait_send()
            far_copy(0, c).wait()
            far_copy(1, c).wait_send()
            relay_copy(c).wait()
            near_copy(1, c, 1, slab).wait_send()
            near_copy(1, c, 1, reader).wait_recv()
        return

    pieces = [
        (1 + c if word < top else 2 * (1 + c), r, c)
        for r, word in enumerate(words)
        for c in chunks
    ]
    pieces.sort()
    for _, r, c in pieces:
        far_copy(r, c).start()
    for offset in offsets:
        own_copy(offset, slab).start()
    local.start()
    for _, r, c in pieces:
        far_copy(r, c).wait_recv()
        for offset in offsets:
            near_copy(r, c, offset, slab).start()
    local.wait()
    for offset in offsets:
        own_copy(offset, slab).wait_send()
        own_copy(offset, sibling(slabs - offset)).wait_recv()
    for _, r, c in pieces:
        far_copy(r, c).wait_send()
        for offset in offsets:
            near_copy(r, c, offset, slab).wait_send()
            near_copy(r, c, offset, sibling(slabs - offset)).wait_recv()


def exchange_call(words, slabs, top, returns):
    width, minutes = returns.shape
    count = chunk_count(slabs)
    vmem = pl.BlockSpec(memory_space=pltpu.VMEM)
    dma = pltpu.SemaphoreType.DMA
    return pl.pallas_call(
        functools.partial(exchange_kernel, words, slabs, top),
        in_specs=[vmem],
        out_specs=[vmem, vmem],
        out_shape=[
            jax.ShapeDtypeStruct((slabs, width // slabs, minutes), returns.dtype),
            jax.ShapeDtypeStruct((ROUNDS, slabs, width, minutes), returns.dtype),
        ],
        scratch_shapes=[
            pltpu.VMEM((width, minutes), returns.dtype), dma((count,)), dma((count,)),
            dma(()), dma((slabs - 1,)), dma((slabs - 1,)),
            dma((ROUNDS, count)), dma((ROUNDS, count)),
            dma((ROUNDS, count, slabs - 1)), dma((ROUNDS, count, slabs - 1)),
        ],
        compiler_params=pltpu.CompilerParams(has_side_effects=True),
    )(returns)


def gram_kernel(bi, own_ref, mates_ref, plan_ref, mask_ref, out_ref, lhs, packed):
    slabs, rows, minutes = own_ref.shape
    width = mates_ref.shape[2]
    total = slabs * minutes
    step = pl.program_id(0)
    block = lax.axis_index("blk")
    factor = float(total) ** (-0.5)
    swap = (plan_ref[0, 0] > plan_ref[1, 0]).astype(jnp.int32)
    groups = width // LANES
    pitch = LAGS * groups * ROUNDS

    start = pl.multiple_of(step * bi, bi)
    own = jnp.concatenate([own_ref[s, pl.ds(start, bi), :] for s in range(slabs)], axis=1)
    own = own.astype(jnp.float32)
    lane = lax.broadcasted_iota(jnp.int32, (bi, total), 1)
    for k in range(LAGS):
        lag = k - LAG
        if lag == 0:
            moved = own
        else:
            moved = pltpu.roll(own, lag % total, 1)
            keep = lane >= lag if lag > 0 else lane < total + lag
            moved = jnp.where(keep, moved, 0.0)
        lhs[k * bi:(k + 1) * bi, :] = moved.astype(lhs.dtype)
    for r in range(ROUNDS):
        partner = jnp.bitwise_xor(block, plan_ref[r, 0])
        scale = mask_ref[block, partner].astype(jnp.float32) * factor
        which = jnp.bitwise_xor(swap, r)
        gram = sum(
            lax.dot_general(
                lhs[:, s * minutes:(s + 1) * minutes], mates_ref[which, s],
                (((1,), (1,)), ((), ())), preferred_element_type=jnp.float32,
            )
            for s in range(slabs)
        ) * scale
        for k in range(LAGS):
            for c in range(groups):
                packed[pl.ds((k * groups + c) * ROUNDS + r, bi, stride=pitch), :] = gram[
                    k * bi:(k + 1) * bi, c * LANES:(c + 1) * LANES
                ]
    out_ref[...] = packed[...].astype(out_ref.dtype)


def gram_call(own, found, plan, pair_mask):
    slabs, rows, minutes = own.shape
    width = found.shape[2]
    total = slabs * minutes
    bi = min(64, rows)
    pitch = LAGS * (width // LANES) * ROUNDS
    whole = lambda a: pl.BlockSpec(a.shape, lambda i: (0,) * a.ndim)
    flat = pl.pallas_call(
        functools.partial(gram_kernel, bi),
        grid=(rows // bi,),
        in_specs=[
            whole(own), whole(found),
            pl.BlockSpec(memory_space=pltpu.SMEM),
            pl.BlockSpec(memory_space=pltpu.SMEM),
        ],
        out_specs=pl.BlockSpec((bi * pitch, LANES), lambda i: (i, 0)),
        out_shape=jax.ShapeDtypeStruct((rows * pitch, LANES), jnp.bfloat16),
        scratch_shapes=[
            pltpu.VMEM((LAGS * bi, total), jnp.bfloat16),
            pltpu.VMEM((bi * pitch, LANES), jnp.float32),
        ],
        compiler_params=pltpu.CompilerParams(vmem_limit_bytes=48 * 2**20),
    )(own, found, plan, pair_mask)
    tiles = flat.reshape(rows, pitch // ROUNDS, ROUNDS, LANES)
    tiles = with_layout_constraint(tiles, Layout(major_to_minor=(0, 1, 2, 3)))
    return tiles.transpose(0, 2, 1, 3).reshape(rows, ROUNDS, LAGS * width)


def choice_kernel(pairs, plan_ref, choice_ref):
    first, second = plan_ref[0, 0], plan_ref[1, 0]
    low, high = jnp.minimum(first, second), jnp.maximum(first, second)
    choice = jnp.int32(0)
    for index, (a, b) in enumerate(pairs):
        choice = jnp.where((low == a) & (high == b), jnp.int32(index), choice)
    choice_ref[0] = choice


def on_device(returns, plan, pair_mask):
    block_count = lax.axis_size("blk")
    slab_count = lax.axis_size("tm")
    pairs = word_pairs(block_count)
    smem = pl.BlockSpec(memory_space=pltpu.SMEM)
    choice = pl.pallas_call(
        functools.partial(choice_kernel, pairs),
        in_specs=[smem],
        out_specs=smem,
        out_shape=jax.ShapeDtypeStruct((1,), jnp.int32),
    )(plan)
    own, found = lax.switch(
        choice[0],
        [
            functools.partial(exchange_call, pair, slab_count, block_count // 2)
            for pair in pairs
        ],
        returns,
    )
    return gram_call(own, found, plan, pair_mask)


def solution(mesh):
    in_specs = (P("blk", "tm"), P(), P())
    out_specs = P(("blk", "tm"), None, None)
    return jax.shard_map(
        on_device, mesh=mesh, in_specs=in_specs, out_specs=out_specs, check_vma=False
    )
```

```python
import functools

import jax
import jax.numpy as jnp
from jax import lax
from jax.experimental import pallas as pl
from jax.experimental.pallas import tpu as pltpu
from jax.experimental.layout import Layout, with_layout_constraint
from jax.sharding import PartitionSpec as P

LAG = 7
LAGS = 2 * LAG + 1
ROUNDS = 2
LANES = 128


def chunk_count(slabs):
    return max(1, 8 // slabs)


def word_pairs(count):
    return [
        (low, high)
        for low in range(1, count)
        for high in range(low, count)
        if low | high == count - 1
    ]


def flipped(block, word):
    bit, partner = 1, block
    while bit <= word:
        if word & bit:
            partner = partner + bit - 2 * bit * ((block // bit) % 2)
        bit *= 2
    return partner


def exchange_kernel(
    words, slabs, top, source, own, mates,
    other, cross_send, cross_recv, local_sem, own_send, own_recv, far_send, far_recv, near_send, near_recv,
):
    block, slab = lax.axis_index("blk"), lax.axis_index("tm")
    width = source.shape[0]
    rows = width // slabs
    count = chunk_count(slabs)
    depth = width // count

    def sibling(offset):
        return (slab + offset) % slabs

    def own_copy(offset, writer):
        reader = sibling(offset)
        return pltpu.make_async_remote_copy(
            src_ref=source.at[pl.ds(pl.multiple_of(reader * rows, rows), rows)],
            dst_ref=own.at[writer],
            send_sem=own_send.at[offset - 1],
            recv_sem=own_recv.at[offset - 1],
            device_id=(block, reader),
            device_id_type=pl.DeviceIdType.MESH,
        )

    def far_copy(r, c):
        return pltpu.make_async_remote_copy(
            src_ref=source.at[pl.ds(c * depth, depth)],
            dst_ref=mates.at[r, slab, pl.ds(c * depth, depth)],
            send_sem=far_send.at[r, c],
            recv_sem=far_recv.at[r, c],
            device_id=(flipped(block, words[r]), slab),
            device_id_type=pl.DeviceIdType.MESH,
        )

    def near_copy(r, c, offset, writer):
        part = pl.ds(c * depth, depth)
        return pltpu.make_async_remote_copy(
            src_ref=mates.at[r, slab, part],
            dst_ref=mates.at[r, writer, part],
            send_sem=near_send.at[r, c, offset - 1],
            recv_sem=near_recv.at[r, c, offset - 1],
            device_id=(block, sibling(offset)),
            device_id_type=pl.DeviceIdType.MESH,
        )

    local = pltpu.make_async_copy(
        source.at[pl.ds(pl.multiple_of(slab * rows, rows), rows)], own.at[slab], local_sem
    )
    offsets = range(1, slabs)
    chunks = range(count)
    if slabs == 2 and words[0] < top // 2:
        reader = sibling(1)

        def cross_copy(c):
            part = pl.ds(c * depth, depth)
            return pltpu.make_async_remote_copy(
                src_ref=source.at[part],
                dst_ref=other.at[part],
                send_sem=cross_send.at[c],
                recv_sem=cross_recv.at[c],
                device_id=(block, reader),
                device_id_type=pl.DeviceIdType.MESH,
            )

        def relay_copy(c):
            part = pl.ds(c * depth, depth)
            return pltpu.make_async_remote_copy(
                src_ref=other.at[part],
                dst_ref=mates.at[0, reader, part],
                send_sem=near_send.at[0, c, 0],
                recv_sem=near_recv.at[0, c, 0],
                device_id=(flipped(block, words[0]), slab),
                device_id_type=pl.DeviceIdType.MESH,
            )

        for c in chunks:
            cross_copy(c).start()
            far_copy(1, c).start()
            far_copy(0, c).start()
        local.start()
        events = [(1 + c, 0, c) for c in chunks] + [(2 * (1 + c), 1, c) for c in chunks]
        for _, r, c in sorted(events):
            if r == 0:
                cross_copy(c).wait_recv()
                relay_copy(c).start()
            else:
                far_copy(1, c).wait_recv()
                near_copy(1, c, 1, slab).start()
        local.wait()
        local_other = pltpu.make_async_copy(
            other.at[pl.ds(pl.multiple_of(slab * rows, rows), rows)], own.at[reader], local_sem
        )
        local_other.start()
        local_other.wait()
        for c in chunks:
            cross_copy(c).wait_send()
            far_copy(0, c).wait()
            far_copy(1, c).wait_send()
            relay_copy(c).wait()
            near_copy(1, c, 1, slab).wait_send()
            near_copy(1, c, 1, reader).wait_recv()
        return

    pieces = [
        (1 + c if word < top else 2 * (1 + c), r, c)
        for r, word in enumerate(words)
        for c in chunks
    ]
    pieces.sort()
    for _, r, c in pieces:
        far_copy(r, c).start()
    for offset in offsets:
        own_copy(offset, slab).start()
    local.start()
    for _, r, c in pieces:
        far_copy(r, c).wait_recv()
        for offset in offsets:
            near_copy(r, c, offset, slab).start()
    local.wait()
    for offset in offsets:
        own_copy(offset, slab).wait_send()
        own_copy(offset, sibling(slabs - offset)).wait_recv()
    for _, r, c in pieces:
        far_copy(r, c).wait_send()
        for offset in offsets:
            near_copy(r, c, offset, slab).wait_send()
            near_copy(r, c, offset, sibling(slabs - offset)).wait_recv()


def exchange_call(words, slabs, top, returns):
    width, minutes = returns.shape
    count = chunk_count(slabs)
    vmem = pl.BlockSpec(memory_space=pltpu.VMEM)
    dma = pltpu.SemaphoreType.DMA
    return pl.pallas_call(
        functools.partial(exchange_kernel, words, slabs, top),
        in_specs=[vmem],
        out_specs=[vmem, vmem],
        out_shape=[
            jax.ShapeDtypeStruct((slabs, width // slabs, minutes), returns.dtype),
            jax.ShapeDtypeStruct((ROUNDS, slabs, width, minutes), returns.dtype),
        ],
        scratch_shapes=[
            pltpu.VMEM((width, minutes), returns.dtype), dma((count,)), dma((count,)),
            dma(()), dma((slabs - 1,)), dma((slabs - 1,)),
            dma((ROUNDS, count)), dma((ROUNDS, count)),
            dma((ROUNDS, count, slabs - 1)), dma((ROUNDS, count, slabs - 1)),
        ],
        compiler_params=pltpu.CompilerParams(has_side_effects=True),
    )(returns)


def gram_kernel(bi, own_ref, mates_ref, plan_ref, mask_ref, out_ref, lhs, packed):
    slabs, rows, minutes = own_ref.shape
    width = mates_ref.shape[2]
    total = slabs * minutes
    step = pl.program_id(0)
    block = lax.axis_index("blk")
    factor = float(total) ** (-0.5)
    swap = (plan_ref[0, 0] > plan_ref[1, 0]).astype(jnp.int32)
    groups = width // LANES
    pitch = LAGS * groups * ROUNDS

    start = pl.multiple_of(step * bi, bi)
    own = jnp.concatenate([own_ref[s, pl.ds(start, bi), :] for s in range(slabs)], axis=1)
    own = own.astype(jnp.float32)
    lane = lax.broadcasted_iota(jnp.int32, (bi, total), 1)
    for k in range(LAGS):
        lag = k - LAG
        if lag == 0:
            moved = own
        else:
            moved = pltpu.roll(own, lag % total, 1)
            keep = lane >= lag if lag > 0 else lane < total + lag
            moved = jnp.where(keep, moved, 0.0)
        lhs[k * bi:(k + 1) * bi, :] = moved.astype(lhs.dtype)
    for r in range(ROUNDS):
        partner = jnp.bitwise_xor(block, plan_ref[r, 0])
        scale = mask_ref[block, partner].astype(jnp.float32) * factor
        which = jnp.bitwise_xor(swap, r)
        gram = sum(
            lax.dot_general(
                lhs[:, s * minutes:(s + 1) * minutes], mates_ref[which, s],
                (((1,), (1,)), ((), ())), preferred_element_type=jnp.float32,
            )
            for s in range(slabs)
        ) * scale
        for k in range(LAGS):
            for c in range(groups):
                packed[pl.ds((k * groups + c) * ROUNDS + r, bi, stride=pitch), :] = gram[
                    k * bi:(k + 1) * bi, c * LANES:(c + 1) * LANES
                ]
    out_ref[...] = packed[...].astype(out_ref.dtype)


def gram_call(own, found, plan, pair_mask):
    slabs, rows, minutes = own.shape
    width = found.shape[2]
    total = slabs * minutes
    bi = min(64, rows)
    pitch = LAGS * (width // LANES) * ROUNDS
    whole = lambda a: pl.BlockSpec(a.shape, lambda i: (0,) * a.ndim)
    flat = pl.pallas_call(
        functools.partial(gram_kernel, bi),
        grid=(rows // bi,),
        in_specs=[
            whole(own), whole(found),
            pl.BlockSpec(memory_space=pltpu.SMEM),
            pl.BlockSpec(memory_space=pltpu.SMEM),
        ],
        out_specs=pl.BlockSpec((bi * pitch, LANES), lambda i: (i, 0)),
        out_shape=jax.ShapeDtypeStruct((rows * pitch, LANES), jnp.bfloat16),
        scratch_shapes=[
            pltpu.VMEM((LAGS * bi, total), jnp.bfloat16),
            pltpu.VMEM((bi * pitch, LANES), jnp.float32),
        ],
        compiler_params=pltpu.CompilerParams(vmem_limit_bytes=48 * 2**20),
    )(own, found, plan, pair_mask)
    tiles = flat.reshape(rows, pitch // ROUNDS, ROUNDS, LANES)
    tiles = with_layout_constraint(tiles, Layout(major_to_minor=(0, 1, 2, 3)))
    return tiles.transpose(0, 2, 1, 3).reshape(rows, ROUNDS, LAGS * width)


def choice_kernel(pairs, plan_ref, choice_ref):
    first, second = plan_ref[0, 0], plan_ref[1, 0]
    low, high = jnp.minimum(first, second), jnp.maximum(first, second)
    choice = jnp.int32(0)
    for index, (a, b) in enumerate(pairs):
        choice = jnp.where((low == a) & (high == b), jnp.int32(index), choice)
    choice_ref[0] = choice


def on_device(returns, plan, pair_mask):
    block_count = lax.axis_size("blk")
    slab_count = lax.axis_size("tm")
    pairs = word_pairs(block_count)
    smem = pl.BlockSpec(memory_space=pltpu.SMEM)
    choice = pl.pallas_call(
        functools.partial(choice_kernel, pairs),
        in_specs=[smem],
        out_specs=smem,
        out_shape=jax.ShapeDtypeStruct((1,), jnp.int32),
    )(plan)
    own, found = lax.switch(
        choice[0],
        [
            functools.partial(exchange_call, pair, slab_count, block_count // 2)
            for pair in pairs
        ],
        returns,
    )
    return gram_call(own, found, plan, pair_mask)


def solution(mesh):
    in_specs = (P("blk", "tm"), P(), P())
    out_specs = P(("blk", "tm"), None, None)
    return jax.shard_map(
        on_device, mesh=mesh, in_specs=in_specs, out_specs=out_specs, check_vma=False
    )
```
